256 devices in a mesh: section: 8 (over z_lo, core), dp: 32 (over z_hi, x, y).
Axes of the slice: x: 4, y: 4, z: 8 (z_hi: 2, z_lo: 4; z = z_hi * 4 + z_lo), core: 2. Of those that a mesh axis runs over, the one named last changes fastest.
Arguments:
- token_grad: bfloat16 [65536, 4608], P(('section', 'dp')), may hold values from -6 to 6
- owner: int32 [65536, 1], P(('section', 'dp')), may hold values from 0 to 255; in each aligned block of 256 rows (0 to 255, 256 to 511, ...) at most 2 rows name the same one
- local_row: int32 [65536], P(('section', 'dp')), may hold values from 0 to 999
Outputs:
- vocab_grad: bfloat16 [256000, 4608], P(('section', 'dp'))
The draws below stay inside these ranges and needn't reach their ends.
Inputs may be any that keep to these rules, and one draw needn't show every extreme that they name: `owner`: among the rows of one device, no shard is named more than 2 times, a bound that some block reaches.
All inputs are finite; a program needn't handle non-finite values.
Results may differ from the reference program's by a relative error of at most 0.001.
Values may be sent and summed in bfloat16 or wider, within the bound.
A program may use at most 64 MiB of HBM per device.

```python
import math
import jax
import jax.numpy as jnp
import numpy as np

D = 4608
VROWS_DEV = 1000
TOK_DEV = 256
CAP = 2
VOCAB = 256000
TOKENS = 65536
N_SECTION = 8
N_DP = 32


def touch_ends(array, key, least, largest):
    place = [jax.random.randint(jax.random.fold_in(key, axis), (), 0, length) for axis, length in enumerate(array.shape)]
    longest = array.shape.index(max(array.shape))
    beside = place[:longest] + [(place[longest] + 1) % array.shape[longest]] + place[longest + 1:]
    return array.at[tuple(place)].set(least).at[tuple(beside)].set(largest)


def level_of(stream_key, shape, pieces, smallest, top_value):
    loudness = 1.0
    for position, blocks in pieces:
        draws = jax.random.uniform(jax.random.fold_in(jax.random.fold_in(stream_key, 6), position), (blocks,), jnp.float32, smallest / len(pieces), top_value / len(pieces))
        loudness = loudness * jnp.repeat(jnp.exp(draws), shape[position] // blocks).reshape((-1,) + (1,) * (len(shape) - 1 - position))
    return loudness


def rank_bounds(count, lean):
    loads = [(1 << 20) // math.isqrt(rank ** lean) + 1 for rank in range(1, count + 1)]
    deviation = 1 + sum(loads) // (1 << 30)
    return np.cumsum(np.array([max(1, weight // deviation) for weight in loads]))


def ranked(stream_key, dims, amount, slope):
    grid = rank_bounds(amount, slope)
    pick = jax.random.randint(jax.random.fold_in(stream_key, 1), dims, 0, int(grid[amount - 1]))
    grade = jnp.searchsorted(jnp.asarray(grid, jnp.int32), pick, side="right")
    return jax.random.permutation(jax.random.fold_in(stream_key, 2), amount)[grade].astype(jnp.int32)


def shared_out(stream_key, own, number, rows, count, top, limit, slope):
    order = jax.random.permutation(stream_key, count)
    packed, usual = portions_of(count, rows * top, limit, slope, True), portions_of(count, rows * top, limit, slope, False)
    places = jnp.arange(count)

    def named(tallies, rotation):
        used = int((tallies > 0).sum())
        fixed = max(1, used // 4)
        moved = fixed + (places - fixed + rotation * (used - fixed)) % max(1, count - fixed)
        return jnp.zeros((count,), jnp.int32).at[order[jnp.where(places < fixed, places, moved)]].set(jnp.asarray(tallies, jnp.int32))

    tallies = jnp.where(number % 4 == 0, named(packed, number // 4), named(usual, number - number // 4 - 1))
    mixed = jax.random.permutation(jax.random.fold_in(own, 3), count)
    source_of, sink = mixed[0:count // 2 * 2:2], mixed[1:count // 2 * 2:2]
    room = jnp.minimum(tallies[source_of] - 1, limit - tallies[sink]) // 2
    room = jnp.where((source_of == order[0]) | (sink == order[0]) | (tallies[sink] == 0), 0, jnp.maximum(room, 0))
    moved = jax.random.randint(jax.random.fold_in(own, 4), (count // 2,), 0, 1 << 20) % (room + 1)
    tallies = tallies.at[source_of].add(-moved).at[sink].add(moved)
    labels = jnp.searchsorted(jnp.cumsum(tallies), jnp.arange(rows * top), side="right").astype(jnp.int32)
    listing = labels.reshape(top, rows).T
    listing = listing[jax.random.permutation(jax.random.fold_in(own, 1), rows)]
    rotation = jax.random.randint(jax.random.fold_in(own, 2), (rows, 1), 0, top)
    return jnp.take_along_axis(listing, (jnp.arange(top)[None, :] + rotation) % top, axis=1)


def portions_of(count, total, most, lean, full):
    loads = [(1 << 20) // math.isqrt(rank ** lean) + 1 for rank in range(1, count + 1)]
    largest = most if full else min(most, max(-(-total // count), total * loads[0] // sum(loads)))
    least = 1 if total - largest >= count - 1 else 0
    counts, surplus = [largest] + [least] * (count - 1), total - largest - least * (count - 1)
    while surplus > 0:
        free = [i for i in range(1, count) if counts[i] < largest] or [i for i in range(1, count) if counts[i] < most]
        pool, budget = sum([loads[i] for i in free]), surplus
        for i in free:
            more = min(most - counts[i], max(1, budget * loads[i] // pool), surplus)
            counts[i] = counts[i] + more
            surplus = surplus - more
    return np.array(counts)


def centred(own_key, extent, deviation, bound, shards=(), dtype=jnp.bfloat16):
    drawn = deviation * jax.random.normal(own_key, extent, jnp.float32)
    if shards:
        drawn = drawn * level_of(own_key, extent, shards, -0.22, 0.18)
    return jnp.clip(drawn, -bound, bound).astype(dtype)


def setup_inputs(seed: int = 0) -> dict:
    splits = jax.random.split(jax.random.key(seed), 4)
    token_grad = centred(splits[0], (TOKENS, D), 1.0, 6.0, ((0, 256),))
    owner_keys = jax.random.split(jax.random.fold_in(splits[1], 1), TOKENS // TOK_DEV)
    owner_turns = jax.random.permutation(jax.random.fold_in(splits[1], 3), TOKENS // TOK_DEV)
    owner = jax.vmap(lambda own, number: shared_out(jax.random.fold_in(splits[1], 2), own, number, TOK_DEV, N_SECTION * N_DP, 1, CAP, 2))(owner_keys, owner_turns).reshape((TOKENS, 1))
    local_row = touch_ends(ranked(splits[2], (TOKENS,), VROWS_DEV, 2), jax.random.fold_in(splits[2], 3), 0, VROWS_DEV - 1).astype(jnp.int32)
    return dict(token_grad=token_grad, owner=owner, local_row=local_row)


def reference(token_grad, owner, local_row):
    vocab_id = (owner[:, 0] * VROWS_DEV + local_row).astype(jnp.int32)
    blocks = []
    for column_start in range(0, D, 512):
        column_end = min(D, column_start + 512)
        piece = token_grad[:, column_start:column_end].astype(jnp.float32)
        summed = jax.ops.segment_sum(piece, vocab_id, num_segments=VOCAB)
        blocks.append(summed.astype(jnp.bfloat16))
    return jnp.concatenate(blocks, axis=1)
```

```python
import functools

import jax
import jax.numpy as jnp
from jax import lax
from jax.experimental import pallas as pl
from jax.experimental.pallas import tpu as pltpu
from jax.sharding import PartitionSpec as P

VROWS_DEV = 1000
Z_HI, Z_LO, CORES = 2, 4, 2
COLUMNS = 512
LANES = 128
MESH = pl.DeviceIdType.MESH
F32, BF16, I32 = jnp.float32, jnp.bfloat16, jnp.int32


def log2(n):
    return n.bit_length() - 1


def kernel(z_n, z_lo_n, core_n, xy_n, cap, x_ref, owner_ref, row_ref, out_ref,
           pack, send, zgot, spread, got, sel2, selector, smeta, zmeta, pmeta, gmeta, stage,
           zs_sem, zr_sem, ps_sem, pr_sem, zm_sem, pm_sem, ms_sem, o_sem):
    chunks, wide = send.shape[0], send.shape[2]
    tokens = x_ref.shape[0]
    p_n = xy_n * core_n
    slab = 2 * z_n
    dp_n = (z_n // z_lo_n) * xy_n
    s, d = lax.axis_index("section"), lax.axis_index("dp")
    my_lo, my_core = s // core_n, s % core_n
    my_hi, my_xy = d // xy_n, d % xy_n
    my_z = my_hi * z_lo_n + my_lo
    my_p = my_xy * core_n + my_core

    def z_peer(k):
        z = (my_z + k) % z_n
        return (z % z_lo_n) * core_n + my_core, (z // z_lo_n) * xy_n + my_xy

    def p_peer(k):
        p = (my_p + k) % p_n
        return my_lo * core_n + p % core_n, my_hi * xy_n + p // core_n

    barrier = pltpu.get_barrier_semaphore()

    def greet_z(k, carry):
        pl.semaphore_signal(barrier, inc=1, device_id=z_peer(k), device_id_type=MESH)
        return carry

    def greet_p(k, carry):
        pl.semaphore_signal(barrier, inc=1, device_id=p_peer(k), device_id_type=MESH)
        return carry

    lax.fori_loop(1, z_n, greet_z, 0)
    lax.fori_loop(1, p_n, greet_p, 0)

    ii = lax.broadcasted_iota(I32, (tokens, tokens), 0)
    jj = lax.broadcasted_iota(I32, (tokens, tokens), 1)

    def to_row(col):
        return jnp.sum(jnp.where(ii == jj, col, 0.0), axis=0, keepdims=True)

    def to_col(row):
        return jnp.sum(jnp.where(ii == jj, row, 0.0), axis=1, keepdims=True)

    own = owner_ref[...]
    own_s, own_d = own >> log2(dp_n), own & (dp_n - 1)
    own_z = (own_d >> log2(xy_n)) * z_lo_n + (own_s >> log2(core_n))
    own_p = (own_d & (xy_n - 1)) * core_n + (own_s & (core_n - 1))
    far = (own_z - my_z + z_n) & (z_n - 1)
    near = (own_p - my_p + p_n) & (p_n - 1)
    own_f, far_f = own.astype(F32), far.astype(F32)
    own_row, far_row = to_row(own_f), to_row(far_f)
    twin = jnp.sum(jnp.where((own_f == own_row) & (jj < ii), 1.0, 0.0), axis=1, keepdims=True)
    place = jnp.sum(jnp.where((far_f == far_row) & (ii < jj), 1.0, 0.0), axis=0, keepdims=True)
    spot = far_row * cap + place
    slots = lax.broadcasted_iota(I32, (z_n * cap, tokens), 0).astype(F32)
    pack[...] = jnp.where(slots == spot, 1.0, 0.0).astype(BF16)
    row = to_col(row_ref[...].astype(F32)).astype(I32)
    lane = lax.broadcasted_iota(I32, (tokens, LANES), 1)
    meta = jnp.where(lane == 0, near.astype(F32), 0.0)
    meta = jnp.where(lane == 1, 2.0 * far_f + twin, meta)
    meta = jnp.where(lane == 2, (row >> 5).astype(F32), meta)
    meta = jnp.where(lane == 3, (row & 31).astype(F32), meta)
    meta = jnp.where(lane == 4, 1.0, meta).astype(BF16)
    packed = jnp.dot(pack[...], meta, preferred_element_type=F32).astype(BF16)
    zmeta[0:cap, :] = packed[0:cap]
    smeta[...] = packed[cap:]

    def z_copy(k, src, dst, ssem, rsem):
        return pltpu.make_async_remote_copy(src, dst, ssem, rsem, device_id=z_peer(k), device_id_type=MESH)

    def p_copy(k, src, dst, ssem, rsem):
        return pltpu.make_async_remote_copy(src, dst, ssem, rsem, device_id=p_peer(k), device_id_type=MESH)

    def pack_chunk(j):
        cols = pl.ds(pl.multiple_of(j * wide, wide), wide)
        part = jnp.dot(pack[...], x_ref[:, cols], preferred_element_type=F32).astype(BF16)
        zgot[j, 0:cap, :] = part[0:cap]
        send[j] = part[cap:]

    order = sorted(range(1, z_n), key=lambda k: -min(k, z_n - k))

    def send_chunk(j):
        for k in order:
            z_copy(k, send.at[j, pl.ds((k - 1) * cap, cap)], zgot.at[j, pl.ds(k * cap, cap)],
                   zs_sem, zr_sem.at[j]).start()

    pack_chunk(0)
    pl.semaphore_wait(barrier, z_n - 1 + p_n - 1)
    for k in order:
        z_copy(k, smeta.at[pl.ds((k - 1) * cap, cap)], zmeta.at[pl.ds(k * cap, cap)], ms_sem, zm_sem).start()
    send_chunk(0)

    def pack_and_send(j, carry):
        pack_chunk(j)
        send_chunk(j)
        return carry

    lax.fori_loop(1, chunks, pack_and_send, 0)

    lane8 = lax.broadcasted_iota(I32, (8, LANES), 1)

    def across(weights, columns):
        w = jnp.zeros((8, LANES), F32)
        for at, value in weights:
            w = jnp.where(lane8 == at, value, w)
        rows = lax.dot_general(w.astype(BF16), columns, (((1,), (1,)), ((), ())), preferred_element_type=F32)
        return rows[0:1] - 1.0

    pltpu.make_async_copy(zmeta.at[pl.ds(cap, (z_n - 1) * cap)], zmeta.at[pl.ds(cap, (z_n - 1) * cap)], zm_sem).wait()
    spot2 = across([(0, float(slab)), (1, 1.0), (4, 1.0)], zmeta[...])
    slots2 = lax.broadcasted_iota(I32, (p_n * slab, z_n * cap), 0).astype(F32)
    sel2[...] = jnp.where(slots2 == spot2, 1.0, 0.0).astype(BF16)
    spread_meta = jnp.dot(sel2[...], zmeta[...], preferred_element_type=F32).astype(BF16)
    gmeta[0:slab, :] = spread_meta[0:slab]
    pmeta[...] = spread_meta[slab:]

    def send_meta(k, carry):
        p_copy(k, pmeta.at[pl.ds((k - 1) * slab, slab)], gmeta.at[pl.ds(k * slab, slab)], ms_sem, pm_sem).start()
        return carry

    rest = (p_n - 1) * slab

    def relay_chunk(j):
        arrived = zgot.at[j, pl.ds(cap, (z_n - 1) * cap)]
        pltpu.make_async_copy(arrived, arrived, zr_sem.at[j]).wait()
        part = jnp.dot(sel2[...], zgot[j], preferred_element_type=F32).astype(BF16)
        got[j, 0:slab, :] = part[0:slab]
        spread[j] = part[slab:]

        def out_to(k, carry):
            p_copy(k, spread.at[j, pl.ds((k - 1) * slab, slab)], got.at[j, pl.ds(k * slab, slab)],
                   ps_sem, pr_sem.at[j]).start()
            return carry

        lax.fori_loop(1, p_n, out_to, 0)

    def out_copy(j):
        return pltpu.make_async_copy(
            stage.at[j], out_ref.at[:, pl.ds(pl.multiple_of(j * wide, wide), wide)], o_sem.at[j])

    def finish_chunk(j):
        arrived = got.at[j, pl.ds(slab, rest)]
        pltpu.make_async_copy(arrived, arrived, pr_sem.at[j]).wait()
        stage[j] = jnp.dot(selector[...], got[j], preferred_element_type=F32).astype(BF16)
        out_copy(j).start()

    lax.fori_loop(1, p_n, send_meta, 0)
    relay_chunk(0)

    arrived = gmeta.at[pl.ds(slab, rest)]
    pltpu.make_async_copy(arrived, arrived, pm_sem).wait()
    mine = across([(2, 32.0), (3, 1.0), (4, 1.0)], gmeta[...])
    vocab = lax.broadcasted_iota(I32, selector.shape, 0).astype(F32)
    selector[...] = jnp.where(vocab == mine, 1.0, 0.0).astype(BF16)

    def step(j, carry):
        relay_chunk(j)
        finish_chunk(j - 1)
        return carry

    lax.fori_loop(1, chunks, step, 0)
    finish_chunk(chunks - 1)

    pltpu.make_async_copy(send, send, zs_sem).wait()
    pltpu.make_async_copy(spread, spread, ps_sem).wait()
    pltpu.make_async_copy(smeta, smeta, ms_sem).wait()
    pltpu.make_async_copy(pmeta, pmeta, ms_sem).wait()

    def drain(j, carry):
        out_copy(j).wait()
        return carry

    lax.fori_loop(0, chunks, drain, 0)


def build(mesh, z_hi, z_lo, cores, vrows, wide):
    section_n, dp_n = mesh.shape["section"], mesh.shape["dp"]
    xy_n = dp_n // z_hi
    z_n, p_n = z_hi * z_lo, xy_n * cores

    def per_device(token_grad, owner, local_row):
        tokens, width = token_grad.shape
        cap = 2 * p_n
        slab = 2 * z_n
        chunks = width // wide
        dma = pltpu.SemaphoreType.DMA
        return pl.pallas_call(
            functools.partial(kernel, z_n, z_lo, cores, xy_n, cap),
            out_shape=jax.ShapeDtypeStruct((vrows, width), BF16),
            in_specs=[pl.BlockSpec(memory_space=pltpu.VMEM)] * 3,
            out_specs=pl.BlockSpec(memory_space=pl.ANY),
            scratch_shapes=[
                pltpu.VMEM((z_n * cap, tokens), BF16),
                pltpu.VMEM((chunks, (z_n - 1) * cap, wide), BF16),
                pltpu.VMEM((chunks, z_n * cap, wide), BF16),
                pltpu.VMEM((chunks, (p_n - 1) * slab, wide), BF16),
                pltpu.VMEM((chunks, p_n * slab, wide), BF16),
                pltpu.VMEM((p_n * slab, z_n * cap), BF16),
                pltpu.VMEM((vrows, p_n * slab), BF16),
                pltpu.VMEM(((z_n - 1) * cap, LANES), BF16),
                pltpu.VMEM((z_n * cap, LANES), BF16),
                pltpu.VMEM(((p_n - 1) * slab, LANES), BF16),
                pltpu.VMEM((p_n * slab, LANES), BF16),
                pltpu.VMEM((chunks, vrows, wide), BF16),
                dma, dma((chunks,)), dma, dma((chunks,)), dma, dma, dma, dma((chunks,)),
            ],
            compiler_params=pltpu.CompilerParams(collective_id=0, has_side_effects=True),
        )(token_grad, owner, local_row.reshape(1, tokens))

    return jax.shard_map(
        per_device,
        mesh=mesh,
        in_specs=(P(("section", "dp"), None), P(("section", "dp"), None), P(("section", "dp"))),
        out_specs=P(("section", "dp"), None),
        check_vma=False,
    )


def solution(mesh):
    return build(mesh, Z_HI, Z_LO, CORES, VROWS_DEV, COLUMNS)
```
